32 devices in a mesh: dom: 2 (over y), loop: 4 (over z), trip: 2 (over x), rep: 2 (over core).
Axes of the slice: x: 2, y: 2, z: 4, core: 2. Of those that a mesh axis runs over, the one named last changes fastest.
Arguments:
- cubic_coupling_slices: bfloat16 [8, 120, 120], P(('dom', 'loop')), parts along dimension 0, may hold values from -6 to 6
- leading_displacement_label: int32 [8], P(('dom', 'loop')), parts along dimension 0, may hold values from 0 to 119
- lattice_shift_pairs: int32 [8, 6], P(('dom', 'loop')), parts along dimension 0, may hold values from 0 to 2
- polarization_vectors: bfloat16 [64, 2, 120, 120], P(('dom', 'trip')), parts along dimension 0, may hold values from -0.5 to 0.5
- mode_pulsations: bfloat16 [64, 120], P(('dom', 'trip')), parts along dimension 0, may hold values from 1 to 4
- momentum_slot_lookup: int32 [64], P('dom'), parts along dimension 0, may hold values from 0 to 31, as said below
- momentum_trios: int32 [64, 3], P(('dom', 'loop', 'trip')), parts along dimension 0, may hold values from 0 to 31, as said below
- thermal_label: int32 [64], P(('dom', 'loop', 'trip')), parts along dimension 0, may hold values from 0 to 7
Outputs:
- strength: float32 [64, 120], P(('dom', 'loop', 'trip'), 'rep'), parts along dimension 0
The draws below stay inside these ranges and needn't reach their ends.
There are 2 independent parts, one for each index of `dom`. The reference program is written for one: setup_inputs(seed, part) draws one part's arguments, and reference() takes and returns one part's arrays. A program takes and returns all parts, laid end to end along the dimension named above; each array names one. Nothing has to cross between parts.
Inputs may be any that keep to these rules, and one draw needn't show every extreme that they name: `momentum_slot_lookup`: each number from 0 to 31 appears once: entry q is the location of q-point q's eigenvectors and frequencies. `momentum_trios`: in each aligned block of 4 rows (the triplets of one device), of the 12 named q-points (repeats counted) at most 12 have momentum_slot_lookup in one range [o * 16, (o + 1) * 16), and exactly 12 fall in some range.
All inputs are finite; a program needn't handle non-finite values.
Results may differ from the reference program's by a relative error of at most 0.00093.
Values may be sent and summed in bfloat16 or wider, within the bound.
A program may use at most 64 MiB of HBM per device.

```python
import math
import jax
import jax.numpy as jnp
from jax import lax

B = 120
QGRID = 8
HEAT_LEVEL_COUNT = 8
TRIP_DEV = 4
Q_DEV = 16
NROWS = 4
PHONON_SET_COUNT = 32
NQ = 32


def qpoint_order(key):
    return jax.random.permutation(jax.random.fold_in(key, 11), NQ).astype(jnp.int32)


def draw_momentum_slot_lookup(key, part):
    return qpoint_order(key)


def draw_momentum_trios(key, part):
    location = qpoint_order(key)
    inverse = jnp.argsort(location).astype(jnp.int32)
    holders = NQ // Q_DEV
    per_device = 3 * TRIP_DEV
    devices = PHONON_SET_COUNT // TRIP_DEV
    capacity = 2 * per_device // holders
    ranking = jnp.arange(per_device, dtype=jnp.int32)
    base_holder = jnp.where(ranking < capacity, 0, 1 + (ranking - capacity) % max(holders - 1, 1)).astype(jnp.int32)
    key_hot = jax.random.fold_in(key, 23)
    key_order = jax.random.fold_in(key, 29)
    key_slot = jax.random.fold_in(key, 31)
    hottest = jax.random.randint(key_hot, (devices, 1), 0, holders).astype(jnp.int32)
    holder_of = (base_holder[None, :] + hottest) % holders
    shuffles = jax.vmap(lambda sub_key: jax.random.permutation(sub_key, per_device))(jax.random.split(key_order, devices))
    holder_of = jnp.take_along_axis(holder_of, shuffles.astype(jnp.int32), axis=1)
    slot_of = jax.random.randint(key_slot, (devices, per_device), 0, Q_DEV).astype(jnp.int32)
    qpoint = inverse[holder_of * Q_DEV + slot_of]
    return qpoint.reshape(PHONON_SET_COUNT, 3).astype(jnp.int32)


def set_ends(entries, stream_key, smallest, top_value):
    extent = entries.shape
    spot = [jax.random.randint(jax.random.fold_in(stream_key, axis), (), 0, extent[axis]) for axis in range(len(extent))]
    entries = entries.at[tuple(spot)].set(smallest)
    longest = extent.index(max(extent))
    spot[longest] = (spot[longest] + 1) % extent[longest]
    return entries.at[tuple(spot)].set(top_value)


def levels(own_key, shape, pieces, least, top_value):
    loudness = 1.0
    for dim, blocks in pieces:
        heights = jax.random.uniform(jax.random.fold_in(jax.random.fold_in(own_key, 6), dim), (blocks,), jnp.float32, least / len(pieces), top_value / len(pieces))
        loudness = loudness * jnp.repeat(jnp.exp(heights), shape[dim] // blocks).reshape((-1,) + (1,) * (len(shape) - 1 - dim))
    return loudness


def noise(own_key, extent, scale, bound, cuts=(), held_as=jnp.bfloat16):
    result = scale * jax.random.normal(own_key, extent, jnp.float32)
    if cuts:
        result = result * levels(own_key, extent, cuts, -0.22, 0.18)
    return jnp.clip(result, -bound, bound).astype(held_as)


def setup_inputs(seed: int = 0, part: int = 0) -> dict:
    streams_of = jax.random.split(jax.random.key(seed), 9)
    part_splits = jax.random.split(jax.random.fold_in(streams_of[8], part), 9)
    cubic_coupling_slices = noise(part_splits[0], (NROWS, B, B), 1.0, 6.0, ((0, 4),))
    leading_displacement_label = set_ends(jax.random.randint(part_splits[1], (NROWS,), 0, B), jax.random.fold_in(part_splits[1], 1), 0, B - 1).astype(jnp.int32)
    lattice_shift_pairs = set_ends(jax.random.randint(part_splits[2], (NROWS, 6), 0, 3), jax.random.fold_in(part_splits[2], 1), 0, 2).astype(jnp.int32)
    polarization_vectors = noise(part_splits[3], (NQ, 2, B, B), B ** -0.5, 0.5, ((0, 2),))
    mode_pulsations = jnp.clip(jnp.exp(math.log(4.0) - 1.3862944 * jax.random.uniform(part_splits[4], (NQ, B), jnp.float32) ** levels(part_splits[4], (NQ, B), ((0, 2),), -0.2, 0.2)), 1.0, 4.0).astype(jnp.bfloat16)
    momentum_slot_lookup = draw_momentum_slot_lookup(jax.random.fold_in(jax.random.fold_in(streams_of[8], part), 71), part)
    momentum_trios = draw_momentum_trios(jax.random.fold_in(jax.random.fold_in(streams_of[8], part), 71), part)
    thermal_label = set_ends(jax.random.randint(part_splits[7], (PHONON_SET_COUNT,), 0, HEAT_LEVEL_COUNT), jax.random.fold_in(part_splits[7], 1), 0, HEAT_LEVEL_COUNT - 1).astype(jnp.int32)
    return dict(cubic_coupling_slices=cubic_coupling_slices, leading_displacement_label=leading_displacement_label, lattice_shift_pairs=lattice_shift_pairs, polarization_vectors=polarization_vectors, mode_pulsations=mode_pulsations, momentum_slot_lookup=momentum_slot_lookup, momentum_trios=momentum_trios, thermal_label=thermal_label)


def grid_coords(qpoint):
    return jnp.stack([qpoint % QGRID, (qpoint // QGRID) % QGRID, (qpoint // (QGRID * QGRID)) % QGRID], axis=-1)


def reference(cubic_coupling_slices, leading_displacement_label, lattice_shift_pairs, polarization_vectors, mode_pulsations, momentum_slot_lookup, momentum_trios, thermal_label):
    flat_rows = cubic_coupling_slices.reshape(NROWS * B, B)
    offsets = lattice_shift_pairs - 1
    thermal_kelvin_list = 0.5 * (thermal_label.astype(jnp.float32) + 1.0)
    scale = 1.0 / (8.0 * B * NROWS)

    def coupling_magnitude(items):
        triple, temper = items
        located = momentum_slot_lookup[triple]
        first_vec = polarization_vectors[located[0]]
        second_vec = polarization_vectors[located[1]]
        third_vec = polarization_vectors[located[2]]
        right_side = third_vec.transpose(1, 0, 2).reshape(B, 2 * B)
        hidden = jnp.dot(flat_rows, right_side, preferred_element_type=jnp.float32).astype(jnp.bfloat16)
        hidden = hidden.reshape(NROWS, B, 2, B).transpose(0, 2, 1, 3).reshape(NROWS, 2 * B, B)
        second_re = second_vec[0].T
        second_im = second_vec[1].T
        mixer = jnp.concatenate([jnp.concatenate([second_re, -second_im], axis=1), jnp.concatenate([second_im, second_re], axis=1)], axis=0)
        mixed = jnp.einsum("ab,sbk->sak", mixer.astype(jnp.float32), hidden.astype(jnp.float32)).astype(jnp.bfloat16)
        mixed = mixed.reshape(NROWS * 2, B * B)
        turns = jnp.sum(offsets[:, :3] * grid_coords(triple[1])[None, :], axis=1) + jnp.sum(offsets[:, 3:] * grid_coords(triple[2])[None, :], axis=1)
        angle = (2.0 * math.pi / QGRID) * jnp.mod(turns, QGRID).astype(jnp.float32)
        cosine = jnp.cos(angle)[:, None]
        sine = jnp.sin(angle)[:, None]
        picked_re = first_vec[0][leading_displacement_label].astype(jnp.float32)
        picked_im = first_vec[1][leading_displacement_label].astype(jnp.float32)
        coef_re = (picked_re * cosine - picked_im * sine).astype(jnp.bfloat16).T
        coef_im = (picked_re * sine + picked_im * cosine).astype(jnp.bfloat16).T
        coeff = jnp.stack([jnp.stack([coef_re, -coef_im], axis=-1), jnp.stack([coef_im, coef_re], axis=-1)], axis=0).reshape(2 * B, 2 * NROWS)
        amplitude = jnp.dot(coeff, mixed, preferred_element_type=jnp.float32)
        power = amplitude[:B] ** 2 + amplitude[B:] ** 2
        first_level = mode_pulsations[located[0]].astype(jnp.float32)
        partner_energy = mode_pulsations[located[1]].astype(jnp.float32)
        closing_energy = mode_pulsations[located[2]].astype(jnp.float32)
        partner_population = 1.0 / jnp.expm1(partner_energy / temper)
        closing_population = 1.0 / jnp.expm1(closing_energy / temper)
        weights = ((1.0 + partner_population[:, None] + closing_population[None, :]) / (partner_energy[:, None] * closing_energy[None, :])).reshape(B * B)
        total = jnp.dot(power, weights, precision=lax.Precision.HIGHEST)
        return total * scale / first_level

    return lax.map(coupling_magnitude, (momentum_trios, thermal_kelvin_list))
```

```python
import functools
import math

import jax
import jax.numpy as jnp
from jax import lax
from jax.experimental import pallas as pl
from jax.experimental.pallas import tpu as pltpu
from jax.sharding import PartitionSpec as P

QGRID = 8


def passed_along(value, axis, steps):
    count = lax.axis_size(axis)
    pairs = [(source, (source + steps) % count) for source in range(count)]
    return lax.ppermute(value, axis, pairs)


def grid_coords(qpoint):
    return jnp.stack(
        [qpoint % QGRID, qpoint // QGRID % QGRID, qpoint // (QGRID * QGRID) % QGRID], axis=-1
    )


def fetched_per_device(
    cubic_coupling_slices,
    leading_displacement_label,
    lattice_shift_pairs,
    polarization_vectors,
    mode_pulsations,
    momentum_slot_lookup,
    momentum_trios,
    thermal_label,
):
    rows_dev = cubic_coupling_slices.shape[0]
    width = cubic_coupling_slices.shape[1]
    trip_dev = momentum_trios.shape[0]
    loop_size = lax.axis_size("loop")
    trip_size = lax.axis_size("trip")
    columns = width // lax.axis_size("rep")
    total_rows = rows_dev * loop_size
    q_held = polarization_vectors.shape[0]
    wanted = momentum_trios.reshape(-1)
    wanted_count = wanted.shape[0]
    catalog = jnp.arange(momentum_slot_lookup.shape[0], dtype=jnp.int32)
    located = jnp.sum(
        jnp.where(wanted[:, None] == catalog[None, :], momentum_slot_lookup[None, :], 0), axis=1
    )
    capacity = 2 * wanted_count // trip_size
    holders = located // q_held
    slots = located % q_held
    ranking = jnp.arange(wanted_count, dtype=jnp.int32)
    earlier = (holders[:, None] == holders[None, :]) & (ranking[None, :] < ranking[:, None])
    position = jnp.sum(earlier.astype(jnp.int32), axis=1)
    matched = (holders[None, None, :] == jnp.arange(trip_size, dtype=jnp.int32)[:, None, None]) & (
        position[None, None, :] == jnp.arange(capacity, dtype=jnp.int32)[None, :, None]
    )
    asking = jnp.sum(jnp.where(matched, slots[None, None, :] + 1, 0), axis=2) - 1
    received = lax.all_to_all(asking, "trip", split_axis=0, concat_axis=0, tiled=True)
    usable = received >= 0
    chosen = jnp.clip(received, 0, q_held - 1)
    sent_blocks = jnp.where(
        usable[:, :, None, None, None],
        polarization_vectors[chosen],
        jnp.zeros((), polarization_vectors.dtype),
    )
    sent_levels = jnp.where(
        usable[:, :, None], mode_pulsations[chosen], jnp.zeros((), mode_pulsations.dtype)
    )
    got_blocks = lax.all_to_all(sent_blocks, "trip", split_axis=0, concat_axis=0, tiled=True)
    got_levels = lax.all_to_all(sent_levels, "trip", split_axis=0, concat_axis=0, tiled=True)
    flat_index = holders * capacity + position
    blocks = got_blocks.reshape((trip_size * capacity,) + got_blocks.shape[2:])[flat_index]
    levels = got_levels.reshape(trip_size * capacity, width)[flat_index]
    blocks = blocks.reshape(trip_dev, 3, 2, width, width)
    levels = levels.reshape(trip_dev, 3, width).astype(jnp.float32)
    first_vec = blocks[:, 0]
    second_vec = blocks[:, 1]
    rep_start = lax.axis_index("rep") * columns
    third_part = lax.dynamic_slice_in_dim(blocks[:, 2], rep_start, columns, 3)
    closing_energy = lax.dynamic_slice_in_dim(levels[:, 2], rep_start, columns, 1)
    right_side = third_part.transpose(2, 0, 1, 3).reshape(width, trip_dev * 2 * columns)
    second_re = jnp.swapaxes(second_vec[:, 0], 1, 2)
    second_im = jnp.swapaxes(second_vec[:, 1], 1, 2)
    mixer = jnp.concatenate(
        [
            jnp.concatenate([second_re, -second_im], axis=2),
            jnp.concatenate([second_im, second_re], axis=2),
        ],
        axis=1,
    )
    second_grid = grid_coords(momentum_trios[:, 1])
    third_grid = grid_coords(momentum_trios[:, 2])
    first_re = first_vec[:, 0]
    first_im = first_vec[:, 1]

    def absorb(force_slab, slab_modes, slab_cells, first_row, stacks):
        mixed_all, coeff_all = stacks
        count = force_slab.shape[0]
        hidden = jnp.dot(
            force_slab.reshape(count * width, width), right_side, preferred_element_type=jnp.float32
        ).astype(jnp.bfloat16)
        hidden = (
            hidden.reshape(count, width, trip_dev, 2, columns)
            .transpose(2, 0, 3, 1, 4)
            .reshape(trip_dev, count, 2 * width, columns)
        )
        mixed = jnp.einsum(
            "tab,tsbk->tsak", mixer, hidden, preferred_element_type=jnp.float32
        ).astype(jnp.bfloat16)
        mixed = mixed.reshape(trip_dev, count * 2, width * columns)
        offsets = slab_cells - 1
        turns = jnp.sum(second_grid[:, None, :] * offsets[None, :, :3], axis=2) + jnp.sum(
            third_grid[:, None, :] * offsets[None, :, 3:], axis=2
        )
        angle = 2.0 * math.pi / QGRID * jnp.mod(turns, QGRID).astype(jnp.float32)
        cosine = jnp.cos(angle)[:, :, None]
        sine = jnp.sin(angle)[:, :, None]
        picked_re = first_re[:, slab_modes, :].astype(jnp.float32)
        picked_im = first_im[:, slab_modes, :].astype(jnp.float32)
        coef_re = jnp.swapaxes((picked_re * cosine - picked_im * sine).astype(jnp.bfloat16), 1, 2)
        coef_im = jnp.swapaxes((picked_re * sine + picked_im * cosine).astype(jnp.bfloat16), 1, 2)
        coeff = jnp.stack(
            [jnp.stack([coef_re, -coef_im], axis=-1), jnp.stack([coef_im, coef_re], axis=-1)],
            axis=1,
        ).reshape(trip_dev, 2 * width, count * 2)
        row_start = first_row * 2
        mixed_all = lax.dynamic_update_slice_in_dim(mixed_all, mixed, row_start, 1)
        coeff_all = lax.dynamic_update_slice_in_dim(coeff_all, coeff, row_start, 2)
        return (mixed_all, coeff_all)

    stacks = (
        jnp.zeros((trip_dev, total_rows * 2, width * columns), jnp.bfloat16),
        jnp.zeros((trip_dev, 2 * width, total_rows * 2), jnp.bfloat16),
    )
    stacks = absorb(
        cubic_coupling_slices, leading_displacement_label, lattice_shift_pairs, 0, stacks
    )

    def advance_both(stop, carried):
        upward, downward, held = carried
        upward = passed_along((upward[0], upward[1], upward[2]), "loop", 1)
        downward = passed_along((downward[0], downward[1], downward[2]), "loop", -1)
        held = absorb(upward[0], upward[1], upward[2], (2 * stop - 1) * rows_dev, held)
        held = absorb(downward[0], downward[1], downward[2], 2 * stop * rows_dev, held)
        return (upward, downward, held)

    starting = (cubic_coupling_slices, leading_displacement_label, lattice_shift_pairs)
    upward, downward, stacks = lax.fori_loop(
        1, loop_size // 2, advance_both, (starting, starting, stacks)
    )
    upward = passed_along((upward[0], upward[1], upward[2]), "loop", 1)
    stacks = absorb(upward[0], upward[1], upward[2], (loop_size - 1) * rows_dev, stacks)
    thermal_kelvin_list = 0.5 * (thermal_label.astype(jnp.float32) + 1.0)
    partner_energy = levels[:, 1]
    partner_population = 1.0 / jnp.expm1(partner_energy / thermal_kelvin_list[:, None])
    closing_population = 1.0 / jnp.expm1(closing_energy / thermal_kelvin_list[:, None])
    weights = (
        (1.0 + partner_population[:, :, None] + closing_population[:, None, :])
        / (partner_energy[:, :, None] * closing_energy[:, None, :])
    ).reshape(trip_dev, width * columns)

    def finish(items):
        mixed_one, coeff_one, weight_one = items
        amplitude = jnp.dot(coeff_one, mixed_one, preferred_element_type=jnp.float32)
        power = amplitude[:width] ** 2 + amplitude[width:] ** 2
        return jnp.dot(power, weight_one, precision=lax.Precision.HIGHEST)

    partial_sums = lax.map(finish, (stacks[0], stacks[1], weights))
    partial_sums = partial_sums * (1.0 / (8.0 * width * total_rows)) / levels[:, 0]
    return lax.psum_scatter(partial_sums, "rep", scatter_dimension=1, tiled=True)


MESH = pl.DeviceIdType.MESH
HALF_ROOT = math.sqrt(0.5)


def pair_list(total_rows):
    return [(a, b) for a in range(total_rows) for b in range(a + 1, total_rows)]


def moved_kernel(
    sizes,
    phi_hbm,
    label_hbm,
    shift_hbm,
    eig_hbm,
    freq_hbm,
    lookup_hbm,
    trio_hbm,
    heat_hbm,
    out_ref,
    phi,
    label,
    shift,
    eig,
    freq,
    lookup,
    trio,
    heat,
    mixer,
    hidden,
    mixed,
    result,
    local_got,
    far_got,
    load_sem,
    row_send,
    row_recv,
    trio_send,
    trio_recv,
    back_send,
    back_recv,
):
    loops, reps, rows_dev, width, trip_dev, q_held = sizes
    half = trip_dev // reps
    total_rows = rows_dev * loops
    columns = width // reps
    here_loop = lax.axis_index("loop")
    here_trip = lax.axis_index("trip")
    here_rep = lax.axis_index("rep")
    other_trip = 1 - here_trip

    loads = [
        pltpu.make_async_copy(src, dst, load_sem.at[n])
        for n, (src, dst) in enumerate(
            [
                (trio_hbm, trio.at[0]),
                (lookup_hbm, lookup),
                (heat_hbm, heat.at[0]),
                (label_hbm, label.at[0]),
                (shift_hbm, shift.at[0]),
                (freq_hbm, freq),
                (eig_hbm, eig),
                (phi_hbm, phi.at[0]),
            ]
        )
    ]
    for load in loads:
        load.start()

    barrier = pltpu.get_barrier_semaphore()
    ups = [lax.rem(here_loop + step, loops) for step in range(1, loops)]
    reps_away = [lax.rem(here_rep + step, reps) for step in range(1, reps)]
    for up in ups:
        pl.semaphore_signal(barrier, inc=1, device_id={"loop": up}, device_id_type=MESH)
    for rep in reps_away:
        pl.semaphore_signal(barrier, inc=1, device_id={"rep": rep}, device_id_type=MESH)
    for rep in [here_rep] + reps_away:
        pl.semaphore_signal(
            barrier, inc=1, device_id={"trip": other_trip, "rep": rep}, device_id_type=MESH
        )
    pl.semaphore_wait(barrier, (loops - 1) + (reps - 1) + reps)

    trio_copies = []
    for n, (src, dst) in enumerate([(trio_hbm, trio.at[1]), (heat_hbm, heat.at[1])]):
        trio_copies.append(
            pltpu.make_async_remote_copy(
                src_ref=src,
                dst_ref=dst,
                send_sem=trio_send.at[n],
                recv_sem=trio_recv.at[n],
                device_id={"trip": other_trip},
                device_id_type=MESH,
            )
        )
    row_copies = []
    for step in range(1, loops):
        for n, (src, dst) in enumerate(
            [
                (label_hbm, label.at[step]),
                (shift_hbm, shift.at[step]),
                (phi_hbm, phi.at[step]),
            ]
        ):
            row_copies.append(
                pltpu.make_async_remote_copy(
                    src_ref=src,
                    dst_ref=dst,
                    send_sem=row_send.at[step, n],
                    recv_sem=row_recv.at[step, n],
                    device_id={"loop": ups[step - 1]},
                    device_id_type=MESH,
                )
            )
    for copy in trio_copies + row_copies:
        copy.start()

    hidden[...] = jnp.zeros_like(hidden)
    mixer[...] = jnp.zeros_like(mixer)
    for load in loads:
        load.wait()
    for copy in trio_copies:
        copy.wait()

    def turned(block):
        return jnp.swapaxes(block.astype(jnp.float32), 0, 1).astype(jnp.bfloat16)

    jobs = []
    for side in range(2):
        for item in range(half):
            row = here_rep * half + item
            points = [trio[side, row, n] for n in range(3)]
            slots = [lax.rem(lookup[point], q_held) for point in points]
            kelvin = 0.5 * (heat[side, row].astype(jnp.float32) + 1.0)
            jobs.append((points, slots, kelvin))

    for n, (points, slots, kelvin) in enumerate(jobs):
        back_re = turned(eig[slots[1], 0])
        back_im = turned(eig[slots[1], 1])
        mixer[n, 0:width, 0:width] = back_re
        mixer[n, 0:width, 128 : 128 + width] = -back_im
        mixer[n, 128 : 128 + width, 0:width] = back_im
        mixer[n, 128 : 128 + width, 128 : 128 + width] = back_re

    for step in range(loops):
        if step:
            for copy in row_copies[3 * (step - 1) : 3 * step]:
                copy.wait_recv()
        for inner in range(rows_dev):
            block = phi[step, inner]
            at = (step * rows_dev + inner) * 128
            for n, (points, slots, kelvin) in enumerate(jobs):
                for part in range(2):
                    hidden[n, part * 128 : part * 128 + width, at : at + width] = jnp.dot(
                        block, eig[slots[2], part], preferred_element_type=jnp.float32
                    ).astype(jnp.bfloat16)

    job_count = len(jobs)
    lanes = lax.broadcasted_iota(jnp.int32, (8, q_held), 1)
    ranks = lax.broadcasted_iota(jnp.int32, (8, q_held), 0)
    picks = []
    for which in range(3):
        wanted = jnp.zeros((8, q_held), jnp.int32)
        for n, (points, slots, kelvin) in enumerate(jobs):
            wanted = jnp.where(ranks == n, slots[which], wanted)
        hot = jnp.where(wanted == lanes, 1.0, 0.0).astype(jnp.bfloat16)
        picks.append(jnp.dot(hot, freq[...], preferred_element_type=jnp.float32))
    temper_ranks = lax.broadcasted_iota(jnp.int32, (8, width), 0)
    temper = jnp.ones((8, width), jnp.float32)
    for n, (points, slots, kelvin) in enumerate(jobs):
        temper = jnp.where(temper_ranks == n, kelvin, temper)
    first_level, second_level, third_level = [
        jnp.where(temper_ranks < job_count, pick, 1.0) for pick in picks
    ]
    second_scale = 1.0 / second_level
    third_scale = 1.0 / third_level
    second_part = (1.0 + 1.0 / (jnp.exp(second_level / temper) - 1.0)) * second_scale
    third_part = third_scale / (jnp.exp(third_level / temper) - 1.0)
    second_scale_col = jnp.swapaxes(second_scale, 0, 1)
    second_part_col = jnp.swapaxes(second_part, 0, 1)
    out_scale = (1.0 / (8.0 * width * total_rows)) / first_level

    pairs = pair_list(total_rows)
    padded_rows = -(-total_rows // 8) * 8
    row_ids = lax.broadcasted_iota(jnp.int32, (padded_rows, width), 0)
    col_ids = lax.broadcasted_iota(jnp.int32, (padded_rows, width), 1)
    named = jnp.zeros((padded_rows, width), jnp.int32)
    for s in range(total_rows):
        named = jnp.where(row_ids == s, label[s // rows_dev, s % rows_dev], named)
    hot_label = jnp.where(named == col_ids, 1.0, 0.0).astype(jnp.bfloat16)

    for n, (points, slots, kelvin) in enumerate(jobs):
        mixed[...] = jnp.dot(mixer[n], hidden[n], preferred_element_type=jnp.float32)
        sums = [None] * (total_rows + 2 * len(pairs))

        def put(index, value):
            sums[index] = value if sums[index] is None else sums[index] + value

        for top in range(0, width, 8):
            weight = (
                second_part_col[top : top + 8, n : n + 1] * third_scale[n : n + 1]
                + second_scale_col[top : top + 8, n : n + 1] * third_part[n : n + 1]
            )
            re = [
                mixed[top : top + 8, s * 128 : s * 128 + width] for s in range(total_rows)
            ]
            im = [
                mixed[128 + top : 136 + top, s * 128 : s * 128 + width]
                for s in range(total_rows)
            ]
            wre = [weight * v for v in re]
            wim = [weight * v for v in im]
            for s in range(total_rows):
                put(s, wre[s] * re[s] + wim[s] * im[s])
            for m, (a, b) in enumerate(pairs):
                put(total_rows + 2 * m, wre[a] * re[b] + wim[a] * im[b])
                put(total_rows + 2 * m + 1, wim[a] * re[b] - wre[a] * im[b])

        turns = jnp.zeros((padded_rows, width), jnp.int32)
        grids = []
        for point in points[1:]:
            grids += [
                lax.rem(point, QGRID),
                lax.rem(lax.div(point, QGRID), QGRID),
                lax.rem(lax.div(point, QGRID * QGRID), QGRID),
            ]
        for s in range(total_rows):
            turn = 0
            for m in range(6):
                turn = turn + grids[m] * (shift[s // rows_dev, s % rows_dev, m] - 1)
            turns = jnp.where(row_ids == s, turn, turns)
        turns = jnp.bitwise_and(turns, QGRID - 1)

        def cosine_of(k):
            k = jnp.bitwise_and(k, QGRID - 1)
            flipped = jnp.minimum(k, QGRID - k)
            return jnp.where(
                flipped == 0,
                1.0,
                jnp.where(
                    flipped == 1,
                    HALF_ROOT,
                    jnp.where(flipped == 2, 0.0, jnp.where(flipped == 3, -HALF_ROOT, -1.0)),
                ),
            ).astype(jnp.float32)

        cosine = cosine_of(turns)
        sine = cosine_of(turns + (QGRID - QGRID // 4))
        picked_re = jnp.dot(hot_label, eig[slots[0], 0], preferred_element_type=jnp.float32)
        picked_im = jnp.dot(hot_label, eig[slots[0], 1], preferred_element_type=jnp.float32)
        coef_re = (
            (picked_re * cosine - picked_im * sine).astype(jnp.bfloat16).astype(jnp.float32)
        )
        coef_im = (
            (picked_re * sine + picked_im * cosine).astype(jnp.bfloat16).astype(jnp.float32)
        )
        total = jnp.zeros((1, width), jnp.float32)
        for index, value in enumerate(sums):
            scalar = jnp.sum(jnp.sum(value, axis=0, keepdims=True), axis=1, keepdims=True)
            if index < total_rows:
                a = slice(index, index + 1)
                term = coef_re[a] * coef_re[a] + coef_im[a] * coef_im[a]
            else:
                a, b = pairs[(index - total_rows) // 2]
                a, b = slice(a, a + 1), slice(b, b + 1)
                if (index - total_rows) % 2 == 0:
                    term = 2.0 * (coef_re[a] * coef_re[b] + coef_im[a] * coef_im[b])
                else:
                    term = -2.0 * (coef_im[a] * coef_re[b] - coef_re[a] * coef_im[b])
            total = total + scalar * term
        side, item = n // half, n % half
        result[side, item : item + 1, 0:width] = total * out_scale[n : n + 1]

    back = []
    for m, step in enumerate(range(1, reps)):
        back.append(
            pltpu.make_async_remote_copy(
                src_ref=result.at[0],
                dst_ref=local_got.at[m],
                send_sem=back_send.at[m],
                recv_sem=back_recv.at[m],
                device_id={"rep": reps_away[m]},
                device_id_type=MESH,
            )
        )
    for step, rep in enumerate([here_rep] + reps_away):
        back.append(
            pltpu.make_async_remote_copy(
                src_ref=result.at[1],
                dst_ref=far_got.at[step],
                send_sem=back_send.at[reps - 1 + step],
                recv_sem=back_recv.at[reps - 1 + step],
                device_id={"trip": other_trip, "rep": rep},
                device_id_type=MESH,
            )
        )
    for copy in back:
        copy.start()
    for copy in back:
        copy.wait()
    for copy in row_copies:
        copy.wait_send()

    near = [result[0, 0:half]] + [local_got[m, 0:half] for m in range(reps - 1)]
    far = [far_got[step, 0:half] for step in range(reps)]
    ordered = []
    for rep in range(reps):
        near_rep, far_rep = near[0], far[0]
        for step in range(1, reps):
            came = lax.rem(here_rep + reps - step, reps) == rep
            near_rep = jnp.where(came, near[step], near_rep)
            far_rep = jnp.where(came, far[step], far_rep)
        for item in range(half):
            point = trio[0, rep * half + item, 0]
            held_here = lax.div(lookup[point], q_held) == here_trip
            ordered.append(
                jnp.where(held_here, near_rep[item : item + 1], far_rep[item : item + 1])
            )
    whole = jnp.concatenate(ordered, axis=0)
    shifted = whole[:, 0:columns]
    for rep in range(1, reps):
        shifted = jnp.where(
            here_rep == rep, whole[:, rep * columns : (rep + 1) * columns], shifted
        )
    out_ref[...] = shifted


def moved_per_device(phi, label, shift, eig, freq, lookup, trio, heat):
    loops, reps = lax.axis_size("loop"), lax.axis_size("rep")
    rows_dev, width = phi.shape[:2]
    trip_dev = trio.shape[0]
    q_held = eig.shape[0]
    total_rows = rows_dev * loops
    half = trip_dev // reps
    jobs = 2 * half
    sizes = (loops, reps, rows_dev, width, trip_dev, q_held)
    dma = pltpu.SemaphoreType.DMA
    half_pad = -(-half // 8) * 8
    return pl.pallas_call(
        functools.partial(moved_kernel, sizes),
        out_shape=jax.ShapeDtypeStruct((trip_dev, width // reps), jnp.float32),
        in_specs=[pl.BlockSpec(memory_space=pl.ANY)] * 8,
        out_specs=pl.BlockSpec(memory_space=pltpu.VMEM),
        scratch_shapes=[
            pltpu.VMEM((loops,) + phi.shape, phi.dtype),
            pltpu.SMEM((loops,) + label.shape, jnp.int32),
            pltpu.SMEM((loops,) + shift.shape, jnp.int32),
            pltpu.VMEM(eig.shape, eig.dtype),
            pltpu.VMEM(freq.shape, freq.dtype),
            pltpu.SMEM(lookup.shape, jnp.int32),
            pltpu.SMEM((2,) + trio.shape, jnp.int32),
            pltpu.SMEM((2,) + heat.shape, jnp.int32),
            pltpu.VMEM((jobs, 256, 256), jnp.bfloat16),
            pltpu.VMEM((jobs, 256, 128 * total_rows), jnp.bfloat16),
            pltpu.VMEM((256, 128 * total_rows), jnp.float32),
            pltpu.VMEM((2, half_pad, 128), jnp.float32),
            pltpu.VMEM((reps - 1, half_pad, 128), jnp.float32),
            pltpu.VMEM((reps, half_pad, 128), jnp.float32),
            dma((8,)),
            dma((loops, 3)),
            dma((loops, 3)),
            dma((2,)),
            dma((2,)),
            dma((2 * reps - 1,)),
            dma((2 * reps - 1,)),
        ],
        compiler_params=pltpu.CompilerParams(collective_id=0, has_side_effects=True),
    )(phi, label, shift, eig, freq, lookup, trio, heat)


def per_device(phi, label, shift, eig, freq, lookup, trio, heat):
    reps = lax.axis_size("rep")
    moved = (
        lax.axis_size("trip") == 2
        and lax.axis_size("loop") * phi.shape[0] <= 8
        and trio.shape[0] % reps == 0
        and reps > 1
        and phi.shape[1] <= 128
        and phi.shape[1] % 8 == 0
    )
    call = moved_per_device if moved else fetched_per_device
    return call(phi, label, shift, eig, freq, lookup, trio, heat)


def solution(mesh):
    in_specs = (
        P(("dom", "loop"), None, None),
        P(("dom", "loop")),
        P(("dom", "loop"), None),
        P(("dom", "trip"), None, None, None),
        P(("dom", "trip"), None),
        P("dom"),
        P(("dom", "loop", "trip"), None),
        P(("dom", "loop", "trip")),
    )
    out_specs = P(("dom", "loop", "trip"), "rep")
    return jax.shard_map(
        per_device, mesh=mesh, in_specs=in_specs, out_specs=out_specs, check_vma=False
    )
```

```python
import functools
import math

import jax
import jax.numpy as jnp
from jax import lax
from jax.experimental import pallas as pl
from jax.experimental.pallas import tpu as pltpu
from jax.sharding import PartitionSpec as P

QGRID = 8


def passed_along(value, axis, steps):
    count = lax.axis_size(axis)
    pairs = [(source, (source + steps) % count) for source in range(count)]
    return lax.ppermute(value, axis, pairs)


def grid_coords(qpoint):
    return jnp.stack(
        [qpoint % QGRID, qpoint // QGRID % QGRID, qpoint // (QGRID * QGRID) % QGRID], axis=-1
    )


def fetched_per_device(
    cubic_coupling_slices,
    leading_displacement_label,
    lattice_shift_pairs,
    polarization_vectors,
    mode_pulsations,
    momentum_slot_lookup,
    momentum_trios,
    thermal_label,
):
    rows_dev = cubic_coupling_slices.shape[0]
    width = cubic_coupling_slices.shape[1]
    trip_dev = momentum_trios.shape[0]
    loop_size = lax.axis_size("loop")
    trip_size = lax.axis_size("trip")
    columns = width // lax.axis_size("rep")
    total_rows = rows_dev * loop_size
    q_held = polarization_vectors.shape[0]
    wanted = momentum_trios.reshape(-1)
    wanted_count = wanted.shape[0]
    catalog = jnp.arange(momentum_slot_lookup.shape[0], dtype=jnp.int32)
    located = jnp.sum(
        jnp.where(wanted[:, None] == catalog[None, :], momentum_slot_lookup[None, :], 0), axis=1
    )
    capacity = 2 * wanted_count // trip_size
    holders = located // q_held
    slots = located % q_held
    ranking = jnp.arange(wanted_count, dtype=jnp.int32)
    earlier = (holders[:, None] == holders[None, :]) & (ranking[None, :] < ranking[:, None])
    position = jnp.sum(earlier.astype(jnp.int32), axis=1)
    matched = (holders[None, None, :] == jnp.arange(trip_size, dtype=jnp.int32)[:, None, None]) & (
        position[None, None, :] == jnp.arange(capacity, dtype=jnp.int32)[None, :, None]
    )
    asking = jnp.sum(jnp.where(matched, slots[None, None, :] + 1, 0), axis=2) - 1
    received = lax.all_to_all(asking, "trip", split_axis=0, concat_axis=0, tiled=True)
    usable = received >= 0
    chosen = jnp.clip(received, 0, q_held - 1)
    sent_blocks = jnp.where(
        usable[:, :, None, None, None],
        polarization_vectors[chosen],
        jnp.zeros((), polarization_vectors.dtype),
    )
    sent_levels = jnp.where(
        usable[:, :, None], mode_pulsations[chosen], jnp.zeros((), mode_pulsations.dtype)
    )
    got_blocks = lax.all_to_all(sent_blocks, "trip", split_axis=0, concat_axis=0, tiled=True)
    got_levels = lax.all_to_all(sent_levels, "trip", split_axis=0, concat_axis=0, tiled=True)
    flat_index = holders * capacity + position
    blocks = got_blocks.reshape((trip_size * capacity,) + got_blocks.shape[2:])[flat_index]
    levels = got_levels.reshape(trip_size * capacity, width)[flat_index]
    blocks = blocks.reshape(trip_dev, 3, 2, width, width)
    levels = levels.reshape(trip_dev, 3, width).astype(jnp.float32)
    first_vec = blocks[:, 0]
    second_vec = blocks[:, 1]
    rep_start = lax.axis_index("rep") * columns
    third_part = lax.dynamic_slice_in_dim(blocks[:, 2], rep_start, columns, 3)
    closing_energy = lax.dynamic_slice_in_dim(levels[:, 2], rep_start, columns, 1)
    right_side = third_part.transpose(2, 0, 1, 3).reshape(width, trip_dev * 2 * columns)
    second_re = jnp.swapaxes(second_vec[:, 0], 1, 2)
    second_im = jnp.swapaxes(second_vec[:, 1], 1, 2)
    mixer = jnp.concatenate(
        [
            jnp.concatenate([second_re, -second_im], axis=2),
            jnp.concatenate([second_im, second_re], axis=2),
        ],
        axis=1,
    )
    second_grid = grid_coords(momentum_trios[:, 1])
    third_grid = grid_coords(momentum_trios[:, 2])
    first_re = first_vec[:, 0]
    first_im = first_vec[:, 1]

    def absorb(force_slab, slab_modes, slab_cells, first_row, stacks):
        mixed_all, coeff_all = stacks
        count = force_slab.shape[0]
        hidden = jnp.dot(
            force_slab.reshape(count * width, width), right_side, preferred_element_type=jnp.float32
        ).astype(jnp.bfloat16)
        hidden = (
            hidden.reshape(count, width, trip_dev, 2, columns)
            .transpose(2, 0, 3, 1, 4)
            .reshape(trip_dev, count, 2 * width, columns)
        )
        mixed = jnp.einsum(
            "tab,tsbk->tsak", mixer, hidden, preferred_element_type=jnp.float32
        ).astype(jnp.bfloat16)
        mixed = mixed.reshape(trip_dev, count * 2, width * columns)
        offsets = slab_cells - 1
        turns = jnp.sum(second_grid[:, None, :] * offsets[None, :, :3], axis=2) + jnp.sum(
            third_grid[:, None, :] * offsets[None, :, 3:], axis=2
        )
        angle = 2.0 * math.pi / QGRID * jnp.mod(turns, QGRID).astype(jnp.float32)
        cosine = jnp.cos(angle)[:, :, None]
        sine = jnp.sin(angle)[:, :, None]
        picked_re = first_re[:, slab_modes, :].astype(jnp.float32)
        picked_im = first_im[:, slab_modes, :].astype(jnp.float32)
        coef_re = jnp.swapaxes((picked_re * cosine - picked_im * sine).astype(jnp.bfloat16), 1, 2)
        coef_im = jnp.swapaxes((picked_re * sine + picked_im * cosine).astype(jnp.bfloat16), 1, 2)
        coeff = jnp.stack(
            [jnp.stack([coef_re, -coef_im], axis=-1), jnp.stack([coef_im, coef_re], axis=-1)],
            axis=1,
        ).reshape(trip_dev, 2 * width, count * 2)
        row_start = first_row * 2
        mixed_all = lax.dynamic_update_slice_in_dim(mixed_all, mixed, row_start, 1)
        coeff_all = lax.dynamic_update_slice_in_dim(coeff_all, coeff, row_start, 2)
        return (mixed_all, coeff_all)

    stacks = (
        jnp.zeros((trip_dev, total_rows * 2, width * columns), jnp.bfloat16),
        jnp.zeros((trip_dev, 2 * width, total_rows * 2), jnp.bfloat16),
    )
    stacks = absorb(
        cubic_coupling_slices, leading_displacement_label, lattice_shift_pairs, 0, stacks
    )

    def advance_both(stop, carried):
        upward, downward, held = carried
        upward = passed_along((upward[0], upward[1], upward[2]), "loop", 1)
        downward = passed_along((downward[0], downward[1], downward[2]), "loop", -1)
        held = absorb(upward[0], upward[1], upward[2], (2 * stop - 1) * rows_dev, held)
        held = absorb(downward[0], downward[1], downward[2], 2 * stop * rows_dev, held)
        return (upward, downward, held)

    starting = (cubic_coupling_slices, leading_displacement_label, lattice_shift_pairs)
    upward, downward, stacks = lax.fori_loop(
        1, loop_size // 2, advance_both, (starting, starting, stacks)
    )
    upward = passed_along((upward[0], upward[1], upward[2]), "loop", 1)
    stacks = absorb(upward[0], upward[1], upward[2], (loop_size - 1) * rows_dev, stacks)
    thermal_kelvin_list = 0.5 * (thermal_label.astype(jnp.float32) + 1.0)
    partner_energy = levels[:, 1]
    partner_population = 1.0 / jnp.expm1(partner_energy / thermal_kelvin_list[:, None])
    closing_population = 1.0 / jnp.expm1(closing_energy / thermal_kelvin_list[:, None])
    weights = (
        (1.0 + partner_population[:, :, None] + closing_population[:, None, :])
        / (partner_energy[:, :, None] * closing_energy[:, None, :])
    ).reshape(trip_dev, width * columns)

    def finish(items):
        mixed_one, coeff_one, weight_one = items
        amplitude = jnp.dot(coeff_one, mixed_one, preferred_element_type=jnp.float32)
        power = amplitude[:width] ** 2 + amplitude[width:] ** 2
        return jnp.dot(power, weight_one, precision=lax.Precision.HIGHEST)

    partial_sums = lax.map(finish, (stacks[0], stacks[1], weights))
    partial_sums = partial_sums * (1.0 / (8.0 * width * total_rows)) / levels[:, 0]
    return lax.psum_scatter(partial_sums, "rep", scatter_dimension=1, tiled=True)


MESH = pl.DeviceIdType.MESH
HALF_ROOT = math.sqrt(0.5)


def pair_list(total_rows):
    return [(a, a + gap) for gap in range(1, total_rows) for a in range(total_rows - gap)]


def moved_kernel(
    sizes,
    phi_hbm,
    label_hbm,
    shift_hbm,
    eig_hbm,
    freq_hbm,
    lookup_hbm,
    trio_hbm,
    heat_hbm,
    out_ref,
    phi,
    label,
    shift,
    eig,
    freq,
    lookup,
    trio,
    heat,
    mixer,
    hidden,
    mixed,
    result,
    local_got,
    far_got,
    load_sem,
    row_send,
    row_recv,
    trio_send,
    trio_recv,
    back_send,
    back_recv,
):
    loops, reps, rows_dev, width, trip_dev, q_held = sizes
    half = trip_dev // reps
    total_rows = rows_dev * loops
    columns = width // reps
    here_loop = lax.axis_index("loop")
    here_trip = lax.axis_index("trip")
    here_rep = lax.axis_index("rep")
    other_trip = 1 - here_trip

    loads = [
        pltpu.make_async_copy(src, dst, load_sem.at[n])
        for n, (src, dst) in enumerate(
            [
                (trio_hbm, trio.at[0]),
                (lookup_hbm, lookup),
                (heat_hbm, heat.at[0]),
                (label_hbm, label.at[0]),
                (shift_hbm, shift.at[0]),
                (freq_hbm, freq),
                (eig_hbm, eig),
                (phi_hbm, phi.at[0]),
            ]
        )
    ]
    barrier = pltpu.get_barrier_semaphore()
    ups = [lax.rem(here_loop + step, loops) for step in range(1, loops)]
    reps_away = [lax.rem(here_rep + step, reps) for step in range(1, reps)]
    for up in ups:
        pl.semaphore_signal(barrier, inc=1, device_id={"loop": up}, device_id_type=MESH)
    for rep in reps_away:
        pl.semaphore_signal(barrier, inc=1, device_id={"rep": rep}, device_id_type=MESH)
    for rep in [here_rep] + reps_away:
        pl.semaphore_signal(
            barrier, inc=1, device_id={"trip": other_trip, "rep": rep}, device_id_type=MESH
        )

    for load in loads:
        load.start()

    pl.semaphore_wait(barrier, (loops - 1) + (reps - 1) + reps)

    trio_copies = []
    for n, (src, dst) in enumerate([(trio_hbm, trio.at[1]), (heat_hbm, heat.at[1])]):
        trio_copies.append(
            pltpu.make_async_remote_copy(
                src_ref=src,
                dst_ref=dst,
                send_sem=trio_send.at[n],
                recv_sem=trio_recv.at[n],
                device_id={"trip": other_trip},
                device_id_type=MESH,
            )
        )
    row_copies = []
    for step in range(1, loops):
        for n, (src, dst) in enumerate(
            [
                (label_hbm, label.at[step]),
                (shift_hbm, shift.at[step]),
                (phi_hbm, phi.at[step]),
            ]
        ):
            row_copies.append(
                pltpu.make_async_remote_copy(
                    src_ref=src,
                    dst_ref=dst,
                    send_sem=row_send.at[step, n],
                    recv_sem=row_recv.at[step, n],
                    device_id={"loop": ups[step - 1]},
                    device_id_type=MESH,
                )
            )
    for copy in trio_copies + row_copies:
        copy.start()

    hidden[...] = jnp.zeros_like(hidden)
    mixer[...] = jnp.zeros_like(mixer)
    for load in loads:
        load.wait()

    def turned(block):
        return jnp.swapaxes(block.astype(jnp.float32), 0, 1).astype(jnp.bfloat16)

    def job_of(side, item):
        row = here_rep * half + item
        points = [trio[side, row, n] for n in range(3)]
        slots = [lax.rem(lookup[point], q_held) for point in points]
        kelvin = 0.5 * (heat[side, row].astype(jnp.float32) + 1.0)
        return points, slots, kelvin

    def set_mixer(n, slots):
        back_re = turned(eig[slots[1], 0])
        back_im = turned(eig[slots[1], 1])
        mixer[n, 0:width, 0:width] = back_re
        mixer[n, 0:width, 128 : 128 + width] = -back_im
        mixer[n, 128 : 128 + width, 0:width] = back_im
        mixer[n, 128 : 128 + width, 128 : 128 + width] = back_re

    def set_hidden(n, slots, step):
        for inner in range(rows_dev):
            at = (step * rows_dev + inner) * 128
            for part in range(2):
                hidden[n, part * 128 : part * 128 + width, at : at + width] = jnp.dot(
                    phi[step, inner], eig[slots[2], part], preferred_element_type=jnp.float32
                ).astype(jnp.bfloat16)

    def set_mixed(n, steps):
        low, high = steps[0] * rows_dev * 128, (steps[-1] + 1) * rows_dev * 128
        mixed[n, :, low:high] = jnp.dot(
            mixer[n], hidden[n, :, low:high], preferred_element_type=jnp.float32
        )

    jobs = [job_of(0, item) for item in range(half)]
    for n, (points, slots, kelvin) in enumerate(jobs):
        set_mixer(n, slots)
        set_hidden(n, slots, 0)

    for copy in trio_copies:
        copy.wait_recv()
    jobs += [job_of(1, item) for item in range(half)]
    for n, (points, slots, kelvin) in enumerate(jobs):
        if n >= half:
            set_mixer(n, slots)
            set_hidden(n, slots, 0)

    job_count = len(jobs)
    lanes = lax.broadcasted_iota(jnp.int32, (8, q_held), 1)
    ranks = lax.broadcasted_iota(jnp.int32, (8, q_held), 0)
    picks = []
    for which in range(3):
        wanted = jnp.zeros((8, q_held), jnp.int32)
        for n, (points, slots, kelvin) in enumerate(jobs):
            wanted = jnp.where(ranks == n, slots[which], wanted)
        hot = jnp.where(wanted == lanes, 1.0, 0.0).astype(jnp.bfloat16)
        picks.append(jnp.dot(hot, freq[...], preferred_element_type=jnp.float32))
    temper_ranks = lax.broadcasted_iota(jnp.int32, (8, width), 0)
    temper = jnp.ones((8, width), jnp.float32)
    for n, (points, slots, kelvin) in enumerate(jobs):
        temper = jnp.where(temper_ranks == n, kelvin, temper)
    first_level, second_level, third_level = [
        jnp.where(temper_ranks < job_count, pick, 1.0) for pick in picks
    ]
    second_scale = 1.0 / second_level
    third_scale = 1.0 / third_level
    second_part = (1.0 + 1.0 / (jnp.exp(second_level / temper) - 1.0)) * second_scale
    third_part = third_scale / (jnp.exp(third_level / temper) - 1.0)
    second_scale_col = jnp.swapaxes(second_scale, 0, 1)
    second_part_col = jnp.swapaxes(second_part, 0, 1)
    out_scale = (1.0 / (8.0 * width * total_rows)) / first_level

    for step in range(1, loops):
        for copy in row_copies[3 * (step - 1) : 3 * step]:
            copy.wait_recv()
        for n, (points, slots, kelvin) in enumerate(jobs):
            set_hidden(n, slots, step)
        if step == loops // 2 - 1:
            for n in range(len(jobs)):
                set_mixed(n, range(loops // 2))
    for n in range(len(jobs)):
        set_mixed(n, range(loops // 2, loops))

    pairs = pair_list(total_rows)
    padded_rows = -(-total_rows // 8) * 8
    row_ids = lax.broadcasted_iota(jnp.int32, (padded_rows, width), 0)
    col_ids = lax.broadcasted_iota(jnp.int32, (padded_rows, width), 1)
    named = jnp.zeros((padded_rows, width), jnp.int32)
    for s in range(total_rows):
        named = jnp.where(row_ids == s, label[s // rows_dev, s % rows_dev], named)
    hot_label = jnp.where(named == col_ids, 1.0, 0.0).astype(jnp.bfloat16)

    for n, (points, slots, kelvin) in enumerate(jobs):
        sums = [None] * (total_rows + 2 * len(pairs))

        def put(index, value):
            sums[index] = value if sums[index] is None else sums[index] + value

        for top in range(0, width, 8):
            weight = (
                second_part_col[top : top + 8, n : n + 1] * third_scale[n : n + 1]
                + second_scale_col[top : top + 8, n : n + 1] * third_part[n : n + 1]
            )
            re = [
                mixed[n, top : top + 8, s * 128 : s * 128 + width] for s in range(total_rows)
            ]
            im = [
                mixed[n, 128 + top : 136 + top, s * 128 : s * 128 + width]
                for s in range(total_rows)
            ]
            wre = [weight * v for v in re]
            wim = [weight * v for v in im]
            for s in range(total_rows):
                put(s, wre[s] * re[s] + wim[s] * im[s])
            for m, (a, b) in enumerate(pairs):
                put(total_rows + m, wre[a] * re[b] + wim[a] * im[b])
                put(total_rows + len(pairs) + m, wim[a] * re[b] - wre[a] * im[b])

        turns = jnp.zeros((padded_rows, width), jnp.int32)
        grids = []
        for point in points[1:]:
            grids += [
                lax.rem(point, QGRID),
                lax.rem(lax.div(point, QGRID), QGRID),
                lax.rem(lax.div(point, QGRID * QGRID), QGRID),
            ]
        for s in range(total_rows):
            turn = 0
            for m in range(6):
                turn = turn + grids[m] * (shift[s // rows_dev, s % rows_dev, m] - 1)
            turns = jnp.where(row_ids == s, turn, turns)
        turns = jnp.bitwise_and(turns, QGRID - 1)

        def cosine_of(k):
            k = jnp.bitwise_and(k, QGRID - 1)
            flipped = jnp.minimum(k, QGRID - k)
            return jnp.where(
                flipped == 0,
                1.0,
                jnp.where(
                    flipped == 1,
                    HALF_ROOT,
                    jnp.where(flipped == 2, 0.0, jnp.where(flipped == 3, -HALF_ROOT, -1.0)),
                ),
            ).astype(jnp.float32)

        cosine = cosine_of(turns)
        sine = cosine_of(turns + (QGRID - QGRID // 4))
        picked_re = jnp.dot(hot_label, eig[slots[0], 0], preferred_element_type=jnp.float32)
        picked_im = jnp.dot(hot_label, eig[slots[0], 1], preferred_element_type=jnp.float32)
        coef_re = (
            (picked_re * cosine - picked_im * sine).astype(jnp.bfloat16).astype(jnp.float32)
        )
        coef_im = (
            (picked_re * sine + picked_im * cosine).astype(jnp.bfloat16).astype(jnp.float32)
        )
        diag = coef_re[0:total_rows] ** 2 + coef_im[0:total_rows] ** 2
        cross_re, cross_im = [], []
        for gap in range(1, total_rows):
            a, b = slice(0, total_rows - gap), slice(gap, total_rows)
            cross_re.append(2.0 * (coef_re[a] * coef_re[b] + coef_im[a] * coef_im[b]))
            cross_im.append(2.0 * (coef_re[a] * coef_im[b] - coef_im[a] * coef_re[b]))
        terms = jnp.concatenate([diag] + cross_re + cross_im, axis=0)
        grams = jnp.concatenate([jnp.sum(v, axis=0, keepdims=True) for v in sums], axis=0)
        grams = jnp.sum(grams, axis=1, keepdims=True)
        total = jnp.sum(grams * terms, axis=0, keepdims=True)
        side, item = n // half, n % half
        result[side, item : item + 1, 0:width] = total * out_scale[n : n + 1]

    back = []
    for m, step in enumerate(range(1, reps)):
        back.append(
            pltpu.make_async_remote_copy(
                src_ref=result.at[0],
                dst_ref=local_got.at[m],
                send_sem=back_send.at[m],
                recv_sem=back_recv.at[m],
                device_id={"rep": reps_away[m]},
                device_id_type=MESH,
            )
        )
    for step, rep in enumerate([here_rep] + reps_away):
        back.append(
            pltpu.make_async_remote_copy(
                src_ref=result.at[1],
                dst_ref=far_got.at[step],
                send_sem=back_send.at[reps - 1 + step],
                recv_sem=back_recv.at[reps - 1 + step],
                device_id={"trip": other_trip, "rep": rep},
                device_id_type=MESH,
            )
        )
    for copy in back:
        copy.start()
    for copy in back:
        copy.wait()
    for copy in trio_copies + row_copies:
        copy.wait_send()

    near = [result[0, 0:half]] + [local_got[m, 0:half] for m in range(reps - 1)]
    far = [far_got[step, 0:half] for step in range(reps)]
    ordered = []
    for rep in range(reps):
        near_rep, far_rep = near[0], far[0]
        for step in range(1, reps):
            came = lax.rem(here_rep + reps - step, reps) == rep
            near_rep = jnp.where(came, near[step], near_rep)
            far_rep = jnp.where(came, far[step], far_rep)
        for item in range(half):
            point = trio[0, rep * half + item, 0]
            held_here = lax.div(lookup[point], q_held) == here_trip
            ordered.append(
                jnp.where(held_here, near_rep[item : item + 1], far_rep[item : item + 1])
            )
    whole = jnp.concatenate(ordered, axis=0)
    shifted = whole[:, 0:columns]
    for rep in range(1, reps):
        shifted = jnp.where(
            here_rep == rep, whole[:, rep * columns : (rep + 1) * columns], shifted
        )
    out_ref[...] = shifted


def moved_per_device(phi, label, shift, eig, freq, lookup, trio, heat):
    loops, reps = lax.axis_size("loop"), lax.axis_size("rep")
    rows_dev, width = phi.shape[:2]
    trip_dev = trio.shape[0]
    q_held = eig.shape[0]
    total_rows = rows_dev * loops
    half = trip_dev // reps
    jobs = 2 * half
    sizes = (loops, reps, rows_dev, width, trip_dev, q_held)
    dma = pltpu.SemaphoreType.DMA
    half_pad = -(-half // 8) * 8
    return pl.pallas_call(
        functools.partial(moved_kernel, sizes),
        out_shape=jax.ShapeDtypeStruct((trip_dev, width // reps), jnp.float32),
        in_specs=[pl.BlockSpec(memory_space=pltpu.HBM)] * 8,
        out_specs=pl.BlockSpec(memory_space=pltpu.VMEM),
        scratch_shapes=[
            pltpu.VMEM((loops,) + phi.shape, phi.dtype),
            pltpu.SMEM((loops,) + label.shape, jnp.int32),
            pltpu.SMEM((loops,) + shift.shape, jnp.int32),
            pltpu.VMEM(eig.shape, eig.dtype),
            pltpu.VMEM(freq.shape, freq.dtype),
            pltpu.SMEM(lookup.shape, jnp.int32),
            pltpu.SMEM((2,) + trio.shape, jnp.int32),
            pltpu.SMEM((2,) + heat.shape, jnp.int32),
            pltpu.VMEM((jobs, 256, 256), jnp.bfloat16),
            pltpu.VMEM((jobs, 256, 128 * total_rows), jnp.bfloat16),
            pltpu.VMEM((jobs, 256, 128 * total_rows), jnp.float32),
            pltpu.VMEM((2, half_pad, 128), jnp.float32),
            pltpu.VMEM((reps - 1, half_pad, 128), jnp.float32),
            pltpu.VMEM((reps, half_pad, 128), jnp.float32),
            dma((8,)),
            dma((loops, 3)),
            dma((loops, 3)),
            dma((2,)),
            dma((2,)),
            dma((2 * reps - 1,)),
            dma((2 * reps - 1,)),
        ],
        compiler_params=pltpu.CompilerParams(collective_id=0, has_side_effects=True),
    )(phi, label, shift, eig, freq, lookup, trio, heat)


def per_device(phi, label, shift, eig, freq, lookup, trio, heat):
    reps = lax.axis_size("rep")
    moved = (
        lax.axis_size("trip") == 2
        and lax.axis_size("loop") >= 4
        and lax.axis_size("loop") * phi.shape[0] <= 8
        and trio.shape[0] % reps == 0
        and reps > 1
        and phi.shape[1] <= 128
        and phi.shape[1] % 8 == 0
    )
    call = moved_per_device if moved else fetched_per_device
    return call(phi, label, shift, eig, freq, lookup, trio, heat)


def solution(mesh):
    in_specs = (
        P(("dom", "loop"), None, None),
        P(("dom", "loop")),
        P(("dom", "loop"), None),
        P(("dom", "trip"), None, None, None),
        P(("dom", "trip"), None),
        P("dom"),
        P(("dom", "loop", "trip"), None),
        P(("dom", "loop", "trip")),
    )
    out_specs = P(("dom", "loop", "trip"), "rep")
    return jax.shard_map(
        per_device, mesh=mesh, in_specs=in_specs, out_specs=out_specs, check_vma=False
    )
```

```python
import functools
import math

import jax
import jax.numpy as jnp
from jax import lax
from jax.experimental import pallas as pl
from jax.experimental.pallas import tpu as pltpu
from jax.sharding import PartitionSpec as P

QGRID = 8


def passed_along(value, axis, steps):
    count = lax.axis_size(axis)
    pairs = [(source, (source + steps) % count) for source in range(count)]
    return lax.ppermute(value, axis, pairs)


def grid_coords(qpoint):
    return jnp.stack(
        [qpoint % QGRID, qpoint // QGRID % QGRID, qpoint // (QGRID * QGRID) % QGRID], axis=-1
    )


def fetched_per_device(
    cubic_coupling_slices,
    leading_displacement_label,
    lattice_shift_pairs,
    polarization_vectors,
    mode_pulsations,
    momentum_slot_lookup,
    momentum_trios,
    thermal_label,
):
    rows_dev = cubic_coupling_slices.shape[0]
    width = cubic_coupling_slices.shape[1]
    trip_dev = momentum_trios.shape[0]
    loop_size = lax.axis_size("loop")
    trip_size = lax.axis_size("trip")
    columns = width // lax.axis_size("rep")
    total_rows = rows_dev * loop_size
    q_held = polarization_vectors.shape[0]
    wanted = momentum_trios.reshape(-1)
    wanted_count = wanted.shape[0]
    catalog = jnp.arange(momentum_slot_lookup.shape[0], dtype=jnp.int32)
    located = jnp.sum(
        jnp.where(wanted[:, None] == catalog[None, :], momentum_slot_lookup[None, :], 0), axis=1
    )
    capacity = 2 * wanted_count // trip_size
    holders = located // q_held
    slots = located % q_held
    ranking = jnp.arange(wanted_count, dtype=jnp.int32)
    earlier = (holders[:, None] == holders[None, :]) & (ranking[None, :] < ranking[:, None])
    position = jnp.sum(earlier.astype(jnp.int32), axis=1)
    matched = (holders[None, None, :] == jnp.arange(trip_size, dtype=jnp.int32)[:, None, None]) & (
        position[None, None, :] == jnp.arange(capacity, dtype=jnp.int32)[None, :, None]
    )
    asking = jnp.sum(jnp.where(matched, slots[None, None, :] + 1, 0), axis=2) - 1
    received = lax.all_to_all(asking, "trip", split_axis=0, concat_axis=0, tiled=True)
    usable = received >= 0
    chosen = jnp.clip(received, 0, q_held - 1)
    sent_blocks = jnp.where(
        usable[:, :, None, None, None],
        polarization_vectors[chosen],
        jnp.zeros((), polarization_vectors.dtype),
    )
    sent_levels = jnp.where(
        usable[:, :, None], mode_pulsations[chosen], jnp.zeros((), mode_pulsations.dtype)
    )
    got_blocks = lax.all_to_all(sent_blocks, "trip", split_axis=0, concat_axis=0, tiled=True)
    got_levels = lax.all_to_all(sent_levels, "trip", split_axis=0, concat_axis=0, tiled=True)
    flat_index = holders * capacity + position
    blocks = got_blocks.reshape((trip_size * capacity,) + got_blocks.shape[2:])[flat_index]
    levels = got_levels.reshape(trip_size * capacity, width)[flat_index]
    blocks = blocks.reshape(trip_dev, 3, 2, width, width)
    levels = levels.reshape(trip_dev, 3, width).astype(jnp.float32)
    first_vec = blocks[:, 0]
    second_vec = blocks[:, 1]
    rep_start = lax.axis_index("rep") * columns
    third_part = lax.dynamic_slice_in_dim(blocks[:, 2], rep_start, columns, 3)
    closing_energy = lax.dynamic_slice_in_dim(levels[:, 2], rep_start, columns, 1)
    right_side = third_part.transpose(2, 0, 1, 3).reshape(width, trip_dev * 2 * columns)
    second_re = jnp.swapaxes(second_vec[:, 0], 1, 2)
    second_im = jnp.swapaxes(second_vec[:, 1], 1, 2)
    mixer = jnp.concatenate(
        [
            jnp.concatenate([second_re, -second_im], axis=2),
            jnp.concatenate([second_im, second_re], axis=2),
        ],
        axis=1,
    )
    second_grid = grid_coords(momentum_trios[:, 1])
    third_grid = grid_coords(momentum_trios[:, 2])
    first_re = first_vec[:, 0]
    first_im = first_vec[:, 1]

    def absorb(force_slab, slab_modes, slab_cells, first_row, stacks):
        mixed_all, coeff_all = stacks
        count = force_slab.shape[0]
        hidden = jnp.dot(
            force_slab.reshape(count * width, width), right_side, preferred_element_type=jnp.float32
        ).astype(jnp.bfloat16)
        hidden = (
            hidden.reshape(count, width, trip_dev, 2, columns)
            .transpose(2, 0, 3, 1, 4)
            .reshape(trip_dev, count, 2 * width, columns)
        )
        mixed = jnp.einsum(
            "tab,tsbk->tsak", mixer, hidden, preferred_element_type=jnp.float32
        ).astype(jnp.bfloat16)
        mixed = mixed.reshape(trip_dev, count * 2, width * columns)
        offsets = slab_cells - 1
        turns = jnp.sum(second_grid[:, None, :] * offsets[None, :, :3], axis=2) + jnp.sum(
            third_grid[:, None, :] * offsets[None, :, 3:], axis=2
        )
        angle = 2.0 * math.pi / QGRID * jnp.mod(turns, QGRID).astype(jnp.float32)
        cosine = jnp.cos(angle)[:, :, None]
        sine = jnp.sin(angle)[:, :, None]
        picked_re = first_re[:, slab_modes, :].astype(jnp.float32)
        picked_im = first_im[:, slab_modes, :].astype(jnp.float32)
        coef_re = jnp.swapaxes((picked_re * cosine - picked_im * sine).astype(jnp.bfloat16), 1, 2)
        coef_im = jnp.swapaxes((picked_re * sine + picked_im * cosine).astype(jnp.bfloat16), 1, 2)
        coeff = jnp.stack(
            [jnp.stack([coef_re, -coef_im], axis=-1), jnp.stack([coef_im, coef_re], axis=-1)],
            axis=1,
        ).reshape(trip_dev, 2 * width, count * 2)
        row_start = first_row * 2
        mixed_all = lax.dynamic_update_slice_in_dim(mixed_all, mixed, row_start, 1)
        coeff_all = lax.dynamic_update_slice_in_dim(coeff_all, coeff, row_start, 2)
        return (mixed_all, coeff_all)

    stacks = (
        jnp.zeros((trip_dev, total_rows * 2, width * columns), jnp.bfloat16),
        jnp.zeros((trip_dev, 2 * width, total_rows * 2), jnp.bfloat16),
    )
    stacks = absorb(
        cubic_coupling_slices, leading_displacement_label, lattice_shift_pairs, 0, stacks
    )

    def advance_both(stop, carried):
        upward, downward, held = carried
        upward = passed_along((upward[0], upward[1], upward[2]), "loop", 1)
        downward = passed_along((downward[0], downward[1], downward[2]), "loop", -1)
        held = absorb(upward[0], upward[1], upward[2], (2 * stop - 1) * rows_dev, held)
        held = absorb(downward[0], downward[1], downward[2], 2 * stop * rows_dev, held)
        return (upward, downward, held)

    starting = (cubic_coupling_slices, leading_displacement_label, lattice_shift_pairs)
    upward, downward, stacks = lax.fori_loop(
        1, loop_size // 2, advance_both, (starting, starting, stacks)
    )
    upward = passed_along((upward[0], upward[1], upward[2]), "loop", 1)
    stacks = absorb(upward[0], upward[1], upward[2], (loop_size - 1) * rows_dev, stacks)
    thermal_kelvin_list = 0.5 * (thermal_label.astype(jnp.float32) + 1.0)
    partner_energy = levels[:, 1]
    partner_population = 1.0 / jnp.expm1(partner_energy / thermal_kelvin_list[:, None])
    closing_population = 1.0 / jnp.expm1(closing_energy / thermal_kelvin_list[:, None])
    weights = (
        (1.0 + partner_population[:, :, None] + closing_population[:, None, :])
        / (partner_energy[:, :, None] * closing_energy[:, None, :])
    ).reshape(trip_dev, width * columns)

    def finish(items):
        mixed_one, coeff_one, weight_one = items
        amplitude = jnp.dot(coeff_one, mixed_one, preferred_element_type=jnp.float32)
        power = amplitude[:width] ** 2 + amplitude[width:] ** 2
        return jnp.dot(power, weight_one, precision=lax.Precision.HIGHEST)

    partial_sums = lax.map(finish, (stacks[0], stacks[1], weights))
    partial_sums = partial_sums * (1.0 / (8.0 * width * total_rows)) / levels[:, 0]
    return lax.psum_scatter(partial_sums, "rep", scatter_dimension=1, tiled=True)


MESH = pl.DeviceIdType.MESH
HALF_ROOT = math.sqrt(0.5)


def pair_list(total_rows):
    return [(a, a + gap) for gap in range(1, total_rows) for a in range(total_rows - gap)]


def moved_kernel(
    sizes,
    phi_hbm,
    label_hbm,
    shift_hbm,
    eig_hbm,
    freq_hbm,
    lookup_hbm,
    trio_hbm,
    heat_hbm,
    out_ref,
    phi,
    label,
    shift,
    eig,
    freq,
    lookup,
    trio,
    heat,
    mixer,
    hidden,
    mixed,
    result,
    local_got,
    far_got,
    load_sem,
    row_send,
    row_recv,
    trio_send,
    trio_recv,
    back_send,
    back_recv,
):
    loops, reps, rows_dev, width, trip_dev, q_held = sizes
    half = trip_dev // reps
    total_rows = rows_dev * loops
    columns = width // reps
    here_loop = lax.axis_index("loop")
    here_trip = lax.axis_index("trip")
    here_rep = lax.axis_index("rep")
    other_trip = 1 - here_trip

    loads = [
        pltpu.make_async_copy(src, dst, load_sem.at[n])
        for n, (src, dst) in enumerate(
            [
                (trio_hbm, trio.at[0]),
                (lookup_hbm, lookup),
                (heat_hbm, heat.at[0]),
                (label_hbm, label.at[0]),
                (shift_hbm, shift.at[0]),
                (freq_hbm, freq),
                (eig_hbm, eig),
                (phi_hbm, phi.at[0]),
            ]
        )
    ]
    barrier = pltpu.get_barrier_semaphore()
    ups = [lax.rem(here_loop + step, loops) for step in range(1, loops)]
    reps_away = [lax.rem(here_rep + step, reps) for step in range(1, reps)]
    for up in ups:
        pl.semaphore_signal(barrier, inc=1, device_id={"loop": up}, device_id_type=MESH)
    for rep in reps_away:
        pl.semaphore_signal(barrier, inc=1, device_id={"rep": rep}, device_id_type=MESH)
    for rep in [here_rep] + reps_away:
        pl.semaphore_signal(
            barrier, inc=1, device_id={"trip": other_trip, "rep": rep}, device_id_type=MESH
        )

    for load in loads:
        load.start()

    pl.semaphore_wait(barrier, (loops - 1) + (reps - 1) + reps)

    trio_copies = []
    for n, (src, dst) in enumerate([(trio_hbm, trio.at[1]), (heat_hbm, heat.at[1])]):
        trio_copies.append(
            pltpu.make_async_remote_copy(
                src_ref=src,
                dst_ref=dst,
                send_sem=trio_send.at[n],
                recv_sem=trio_recv.at[n],
                device_id={"trip": other_trip},
                device_id_type=MESH,
            )
        )
    row_copies = []
    for step in range(1, loops):
        for n, (src, dst) in enumerate(
            [
                (label_hbm, label.at[step]),
                (shift_hbm, shift.at[step]),
                (phi_hbm, phi.at[step]),
            ]
        ):
            row_copies.append(
                pltpu.make_async_remote_copy(
                    src_ref=src,
                    dst_ref=dst,
                    send_sem=row_send.at[step, n],
                    recv_sem=row_recv.at[step, n],
                    device_id={"loop": ups[step - 1]},
                    device_id_type=MESH,
                )
            )
    for copy in trio_copies + row_copies:
        copy.start()

    hidden[...] = jnp.zeros_like(hidden)
    mixer[...] = jnp.zeros_like(mixer)
    for load in loads:
        load.wait()

    def turned(block):
        return jnp.swapaxes(block.astype(jnp.float32), 0, 1).astype(jnp.bfloat16)

    def job_of(side, item):
        row = here_rep * half + item
        points = [trio[side, row, n] for n in range(3)]
        slots = [lax.rem(lookup[point], q_held) for point in points]
        kelvin = 0.5 * (heat[side, row].astype(jnp.float32) + 1.0)
        return points, slots, kelvin

    def set_mixer(n, slots):
        back_re = turned(eig[slots[1], 0])
        back_im = turned(eig[slots[1], 1])
        mixer[n, 0:width, 0:width] = back_re
        mixer[n, 0:width, 128 : 128 + width] = -back_im
        mixer[n, 128 : 128 + width, 0:width] = back_im
        mixer[n, 128 : 128 + width, 128 : 128 + width] = back_re

    def set_hidden(n, slots, step):
        for inner in range(rows_dev):
            at = (step * rows_dev + inner) * 128
            for part in range(2):
                hidden[n, part * 128 : part * 128 + width, at : at + width] = jnp.dot(
                    phi[step, inner], eig[slots[2], part], preferred_element_type=jnp.float32
                ).astype(jnp.bfloat16)

    def set_mixed(n, steps):
        low, high = steps[0] * rows_dev * 128, (steps[-1] + 1) * rows_dev * 128
        mixed[n, :, low:high] = jnp.dot(
            mixer[n], hidden[n, :, low:high], preferred_element_type=jnp.float32
        )

    jobs = [job_of(0, item) for item in range(half)]
    for n, (points, slots, kelvin) in enumerate(jobs):
        set_mixer(n, slots)
        set_hidden(n, slots, 0)

    for copy in trio_copies:
        copy.wait_recv()
    jobs += [job_of(1, item) for item in range(half)]
    for n, (points, slots, kelvin) in enumerate(jobs):
        if n >= half:
            set_mixer(n, slots)
            set_hidden(n, slots, 0)

    job_count = len(jobs)
    lanes = lax.broadcasted_iota(jnp.int32, (8, q_held), 1)
    ranks = lax.broadcasted_iota(jnp.int32, (8, q_held), 0)
    picks = []
    for which in range(3):
        wanted = jnp.zeros((8, q_held), jnp.int32)
        for n, (points, slots, kelvin) in enumerate(jobs):
            wanted = jnp.where(ranks == n, slots[which], wanted)
        hot = jnp.where(wanted == lanes, 1.0, 0.0).astype(jnp.bfloat16)
        picks.append(jnp.dot(hot, freq[...], preferred_element_type=jnp.float32))
    temper_ranks = lax.broadcasted_iota(jnp.int32, (8, width), 0)
    temper = jnp.ones((8, width), jnp.float32)
    for n, (points, slots, kelvin) in enumerate(jobs):
        temper = jnp.where(temper_ranks == n, kelvin, temper)
    first_level, second_level, third_level = [
        jnp.where(temper_ranks < job_count, pick, 1.0) for pick in picks
    ]
    second_scale = 1.0 / second_level
    third_scale = 1.0 / third_level
    second_part = (1.0 + 1.0 / (jnp.exp(second_level / temper) - 1.0)) * second_scale
    third_part = third_scale / (jnp.exp(third_level / temper) - 1.0)
    second_scale_col = jnp.swapaxes(second_scale, 0, 1)
    second_part_col = jnp.swapaxes(second_part, 0, 1)
    out_scale = (1.0 / (8.0 * width * total_rows)) / first_level

    for step in range(1, loops):
        for copy in row_copies[3 * (step - 1) : 3 * step]:
            copy.wait_recv()
        for n, (points, slots, kelvin) in enumerate(jobs):
            set_hidden(n, slots, step)
        if step == loops // 2 - 1:
            for n in range(len(jobs)):
                set_mixed(n, range(loops // 2))
    for n in range(len(jobs)):
        set_mixed(n, range(loops // 2, loops))

    pairs = pair_list(total_rows)
    padded_rows = -(-total_rows // 8) * 8
    row_ids = lax.broadcasted_iota(jnp.int32, (padded_rows, width), 0)
    col_ids = lax.broadcasted_iota(jnp.int32, (padded_rows, width), 1)
    named = jnp.zeros((padded_rows, width), jnp.int32)
    for s in range(total_rows):
        named = jnp.where(row_ids == s, label[s // rows_dev, s % rows_dev], named)
    hot_label = jnp.where(named == col_ids, 1.0, 0.0).astype(jnp.bfloat16)

    def finish(n, points, slots):
        sums = [None] * (total_rows + 2 * len(pairs))

        def put(index, value):
            sums[index] = value if sums[index] is None else sums[index] + value

        for top in range(0, width, 8):
            weight = (
                second_part_col[top : top + 8, n : n + 1] * third_scale[n : n + 1]
                + second_scale_col[top : top + 8, n : n + 1] * third_part[n : n + 1]
            )
            re = [
                mixed[n, top : top + 8, s * 128 : s * 128 + width] for s in range(total_rows)
            ]
            im = [
                mixed[n, 128 + top : 136 + top, s * 128 : s * 128 + width]
                for s in range(total_rows)
            ]
            wre = [weight * v for v in re]
            wim = [weight * v for v in im]
            for s in range(total_rows):
                put(s, wre[s] * re[s] + wim[s] * im[s])
            for m, (a, b) in enumerate(pairs):
                put(total_rows + m, wre[a] * re[b] + wim[a] * im[b])
                put(total_rows + len(pairs) + m, wim[a] * re[b] - wre[a] * im[b])

        turns = jnp.zeros((padded_rows, width), jnp.int32)
        grids = []
        for point in points[1:]:
            grids += [
                lax.rem(point, QGRID),
                lax.rem(lax.div(point, QGRID), QGRID),
                lax.rem(lax.div(point, QGRID * QGRID), QGRID),
            ]
        for s in range(total_rows):
            turn = 0
            for m in range(6):
                turn = turn + grids[m] * (shift[s // rows_dev, s % rows_dev, m] - 1)
            turns = jnp.where(row_ids == s, turn, turns)
        turns = jnp.bitwise_and(turns, QGRID - 1)

        def cosine_of(k):
            k = jnp.bitwise_and(k, QGRID - 1)
            flipped = jnp.minimum(k, QGRID - k)
            return jnp.where(
                flipped == 0,
                1.0,
                jnp.where(
                    flipped == 1,
                    HALF_ROOT,
                    jnp.where(flipped == 2, 0.0, jnp.where(flipped == 3, -HALF_ROOT, -1.0)),
                ),
            ).astype(jnp.float32)

        cosine = cosine_of(turns)
        sine = cosine_of(turns + (QGRID - QGRID // 4))
        picked_re = jnp.dot(hot_label, eig[slots[0], 0], preferred_element_type=jnp.float32)
        picked_im = jnp.dot(hot_label, eig[slots[0], 1], preferred_element_type=jnp.float32)
        coef_re = (
            (picked_re * cosine - picked_im * sine).astype(jnp.bfloat16).astype(jnp.float32)
        )
        coef_im = (
            (picked_re * sine + picked_im * cosine).astype(jnp.bfloat16).astype(jnp.float32)
        )
        diag = coef_re[0:total_rows] ** 2 + coef_im[0:total_rows] ** 2
        cross_re, cross_im = [], []
        for gap in range(1, total_rows):
            a, b = slice(0, total_rows - gap), slice(gap, total_rows)
            cross_re.append(2.0 * (coef_re[a] * coef_re[b] + coef_im[a] * coef_im[b]))
            cross_im.append(2.0 * (coef_re[a] * coef_im[b] - coef_im[a] * coef_re[b]))
        terms = jnp.concatenate([diag] + cross_re + cross_im, axis=0)
        grams = jnp.concatenate([jnp.sum(v, axis=0, keepdims=True) for v in sums], axis=0)
        grams = jnp.sum(grams, axis=1, keepdims=True)
        total = jnp.sum(grams * terms, axis=0, keepdims=True)
        side, item = n // half, n % half
        result[side, item : item + 1, 0:width] = total * out_scale[n : n + 1]

    for n in range(half, 2 * half):
        finish(n, jobs[n][0], jobs[n][1])
    back = []
    for step, rep in enumerate([here_rep] + reps_away):
        back.append(
            pltpu.make_async_remote_copy(
                src_ref=result.at[1],
                dst_ref=far_got.at[step],
                send_sem=back_send.at[reps - 1 + step],
                recv_sem=back_recv.at[reps - 1 + step],
                device_id={"trip": other_trip, "rep": rep},
                device_id_type=MESH,
            )
        )
    for copy in back:
        copy.start()
    for n in range(half):
        finish(n, jobs[n][0], jobs[n][1])
    for m, step in enumerate(range(1, reps)):
        back.append(
            pltpu.make_async_remote_copy(
                src_ref=result.at[0],
                dst_ref=local_got.at[m],
                send_sem=back_send.at[m],
                recv_sem=back_recv.at[m],
                device_id={"rep": reps_away[m]},
                device_id_type=MESH,
            )
        )
    for copy in back[reps:]:
        copy.start()
    for copy in back:
        copy.wait()
    for copy in trio_copies + row_copies:
        copy.wait_send()

    near = [result[0, 0:half]] + [local_got[m, 0:half] for m in range(reps - 1)]
    far = [far_got[step, 0:half] for step in range(reps)]
    ordered = []
    for rep in range(reps):
        near_rep, far_rep = near[0], far[0]
        for step in range(1, reps):
            came = lax.rem(here_rep + reps - step, reps) == rep
            near_rep = jnp.where(came, near[step], near_rep)
            far_rep = jnp.where(came, far[step], far_rep)
        for item in range(half):
            point = trio[0, rep * half + item, 0]
            held_here = lax.div(lookup[point], q_held) == here_trip
            ordered.append(
                jnp.where(held_here, near_rep[item : item + 1], far_rep[item : item + 1])
            )
    whole = jnp.concatenate(ordered, axis=0)
    shifted = whole[:, 0:columns]
    for rep in range(1, reps):
        shifted = jnp.where(
            here_rep == rep, whole[:, rep * columns : (rep + 1) * columns], shifted
        )
    out_ref[...] = shifted


def moved_per_device(phi, label, shift, eig, freq, lookup, trio, heat):
    loops, reps = lax.axis_size("loop"), lax.axis_size("rep")
    rows_dev, width = phi.shape[:2]
    trip_dev = trio.shape[0]
    q_held = eig.shape[0]
    total_rows = rows_dev * loops
    half = trip_dev // reps
    jobs = 2 * half
    sizes = (loops, reps, rows_dev, width, trip_dev, q_held)
    dma = pltpu.SemaphoreType.DMA
    half_pad = -(-half // 8) * 8
    return pl.pallas_call(
        functools.partial(moved_kernel, sizes),
        out_shape=jax.ShapeDtypeStruct((trip_dev, width // reps), jnp.float32),
        in_specs=[pl.BlockSpec(memory_space=pltpu.HBM)] * 8,
        out_specs=pl.BlockSpec(memory_space=pltpu.VMEM),
        scratch_shapes=[
            pltpu.VMEM((loops,) + phi.shape, phi.dtype),
            pltpu.SMEM((loops,) + label.shape, jnp.int32),
            pltpu.SMEM((loops,) + shift.shape, jnp.int32),
            pltpu.VMEM(eig.shape, eig.dtype),
            pltpu.VMEM(freq.shape, freq.dtype),
            pltpu.SMEM(lookup.shape, jnp.int32),
            pltpu.SMEM((2,) + trio.shape, jnp.int32),
            pltpu.SMEM((2,) + heat.shape, jnp.int32),
            pltpu.VMEM((jobs, 256, 256), jnp.bfloat16),
            pltpu.VMEM((jobs, 256, 128 * total_rows), jnp.bfloat16),
            pltpu.VMEM((jobs, 256, 128 * total_rows), jnp.float32),
            pltpu.VMEM((2, half_pad, 128), jnp.float32),
            pltpu.VMEM((reps - 1, half_pad, 128), jnp.float32),
            pltpu.VMEM((reps, half_pad, 128), jnp.float32),
            dma((8,)),
            dma((loops, 3)),
            dma((loops, 3)),
            dma((2,)),
            dma((2,)),
            dma((2 * reps - 1,)),
            dma((2 * reps - 1,)),
        ],
        compiler_params=pltpu.CompilerParams(collective_id=0, has_side_effects=True),
    )(phi, label, shift, eig, freq, lookup, trio, heat)


def per_device(phi, label, shift, eig, freq, lookup, trio, heat):
    reps = lax.axis_size("rep")
    moved = (
        lax.axis_size("trip") == 2
        and lax.axis_size("loop") >= 4
        and lax.axis_size("loop") * phi.shape[0] <= 8
        and trio.shape[0] % reps == 0
        and reps > 1
        and phi.shape[1] <= 128
        and phi.shape[1] % 8 == 0
    )
    call = moved_per_device if moved else fetched_per_device
    return call(phi, label, shift, eig, freq, lookup, trio, heat)


def solution(mesh):
    in_specs = (
        P(("dom", "loop"), None, None),
        P(("dom", "loop")),
        P(("dom", "loop"), None),
        P(("dom", "trip"), None, None, None),
        P(("dom", "trip"), None),
        P("dom"),
        P(("dom", "loop", "trip"), None),
        P(("dom", "loop", "trip")),
    )
    out_specs = P(("dom", "loop", "trip"), "rep")
    return jax.shard_map(
        per_device, mesh=mesh, in_specs=in_specs, out_specs=out_specs, check_vma=False
    )
```
